128 devices in a mesh: gx: 8 (over y, x_lo), gy: 16 (over z, x_hi, core).
Axes of the slice: x: 4 (x_hi: 2, x_lo: 2; x = x_hi * 2 + x_lo), y: 4, z: 4, core: 2. Of those that a mesh axis runs over, the one named last changes fastest.
Arguments:
- hidden_in: bfloat16 [8192, 2048], P('gx', 'gy'), may hold values from -1.05 to 1.05
- gain_attn: float32 [2048], replicated, may hold values from 0.5 to 1.5
- gain_ffn: float32 [2048], replicated, may hold values from 0.5 to 1.5
- w_query: bfloat16 [2048, 2048], P(None, 'gy'), may hold values from -0.125 to 0.125
- w_key: bfloat16 [2048, 2048], P(None, 'gy'), may hold values from -0.0234375 to 0.0234375
- w_value: bfloat16 [2048, 2048], P(None, 'gy'), may hold values from -0.125 to 0.125
- w_out: bfloat16 [2048, 2048], P('gy'), may hold values from -0.5 to 0.5
- w_in: bfloat16 [2048, 10240], P(None, 'gy'), may hold values from -0.125 to 0.125
- w_down: bfloat16 [5120, 2048], P('gy'), may hold values from -0.078125 to 0.078125
- rel_bias: float32 [32, 32], replicated, may hold values from -4 to 4
- kv_cache: bfloat16 [8192, 2, 2048], P('gx', None, 'gy'), may hold values from -21 to 21
- segment_ids: int32 [8192], P('gx'), may hold values from -1 to 8128, as said below
- kv_owner: int32 [8192], P('gx'), may hold values from 0 to 7, as said below
- kv_slot: int32 [8192], P('gx'), may hold values from 0 to 1023, as said below
Outputs:
- output: float32 [8192, 2048], P('gx', 'gy')
- kv_pool: bfloat16 [8192, 2, 2048], P('gx', None, 'gy')
The draws below stay inside these ranges and needn't reach their ends.
Inputs may be any that keep to these rules, and one draw needn't show every extreme that they name: `segment_ids`: each aligned block of 1024 rows holds whole segments of 64 to 1024 rows and padding rows marked -1; a segment's id is the index of its first row; segment 0 is exactly the first 512 rows; the last 64 rows form one segment. `kv_owner`: each aligned block of 1024 rows names every owner exactly 128 times. No two rows share both kv_owner and kv_slot.
All inputs are finite; a program needn't handle non-finite values.
Results may differ from the reference program's by a relative error of at most 0.017.
Values may be sent and summed in bfloat16 or wider, within the bound.
No kernel may reach another device: no remote copies, remote signals or barrier semaphores. Data moves between devices by JAX's collectives and lax.ppermute only.
A program may use at most 128 MiB of HBM per device.

```python
import math
import jax
import jax.numpy as jnp
import numpy as np
from jax import lax

D = 2048
HEADS = 32
DK = 64
FF = 5120
BUCKETS = 32
TOK_GX = 1024
CONT = 512
SEG_MIN = 64
HD = 2048
SEG_MAX = 1024
NEW = 8192
CACHE = 8192
SEND = 128
N_GY = 16


def draw_hidden_in(key, part):
    key_a, key_b, key_c = jax.random.split(key, 3)
    row_scale = jnp.exp(jax.random.uniform(key_b, (NEW, 1), jnp.float32, -0.69, 0.47))
    col_scale = jnp.exp(jax.random.uniform(key_c, (1, D), jnp.float32, -0.69, 0.47))
    noise = jnp.clip(jax.random.normal(key_a, (NEW, D), jnp.float32), -4.0, 4.0)
    return (0.1 * noise * row_scale * col_scale).astype(jnp.bfloat16)


def draw_kv_cache(key, part):
    key_a = jax.random.fold_in(key, 0)
    key_c = jax.random.fold_in(key, 2)
    key_rows = 0.19 * jnp.clip(jax.random.normal(key_a, (CACHE, HD), jnp.float32), -6.0, 6.0)
    value_rows = jnp.clip(jax.random.normal(key_c, (CACHE, HD), jnp.float32), -6.0, 6.0)
    return jnp.stack([key_rows, value_rows], axis=1).astype(jnp.bfloat16)


def draw_segment_ids(key, part):
    blocks = NEW // TOK_GX
    most_segments = TOK_GX // SEG_MIN + 1
    lengths = jax.random.randint(jax.random.fold_in(key, 3), (blocks, most_segments), SEG_MIN, SEG_MAX + 1)
    lengths = lengths.at[0, 0].set(CONT)
    ends = jnp.cumsum(lengths, axis=1)
    starts = ends - lengths
    row_ids = jnp.arange(TOK_GX)
    which = jnp.sum((starts[:, None, :] <= row_ids[None, :, None]).astype(jnp.int32), axis=2) - 1
    start_of = jnp.take_along_axis(starts, which, axis=1)
    end_of = jnp.take_along_axis(ends, which, axis=1)
    first_rows = jnp.arange(blocks)[:, None] * TOK_GX + start_of
    room = jnp.where(jnp.arange(blocks) == blocks - 1, TOK_GX - SEG_MIN, TOK_GX)[:, None]
    seg_ids = jnp.where(end_of <= room, first_rows, -1)
    tail = (jnp.arange(blocks)[:, None] == blocks - 1) & (row_ids[None, :] >= TOK_GX - SEG_MIN)
    seg_ids = jnp.where(tail, NEW - SEG_MIN, seg_ids)
    return seg_ids.reshape(NEW).astype(jnp.int32)


def permute_rows(sub_key):
    return jax.random.permutation(sub_key, TOK_GX)


def owner_and_slot(key):
    base_key = jax.random.fold_in(key, 17)
    blocks = NEW // TOK_GX
    row_keys = jax.random.split(jax.random.fold_in(base_key, 1), blocks)
    row_perms = jax.vmap(permute_rows)(row_keys)
    owners = row_perms // SEND
    send_rank = row_perms % SEND
    slot_keys = jax.random.split(jax.random.fold_in(base_key, 2), blocks)
    slot_perms = jax.vmap(permute_rows)(slot_keys)
    sources = jnp.arange(blocks)[:, None]
    slots = slot_perms[owners, sources * SEND + send_rank]
    return (owners.reshape(NEW).astype(jnp.int32), slots.reshape(NEW).astype(jnp.int32))


def draw_kv_owner(key, part):
    return owner_and_slot(key)[0]


def draw_kv_slot(key, part):
    return owner_and_slot(key)[1]


def level_of(own_key, shape, cuts, low, largest):
    level, own = 1.0, jax.random.fold_in(own_key, 6)
    for position, blocks in cuts:
        draws = jnp.exp(jax.random.uniform(jax.random.fold_in(own, position), (blocks,), jnp.float32, low / len(cuts), largest / len(cuts)))
        level = level * jnp.repeat(draws, shape[position] // blocks).reshape([-1 if axis == position else 1 for axis in range(len(shape))])
    return level


def scatter_about(own_key, dims, spread, most, pieces=(), held_as=jnp.bfloat16):
    factor_of = level_of(own_key, dims, pieces, -0.22, 0.18) if pieces else 1.0
    drawn = jax.random.normal(own_key, dims, jnp.float32) * spread * factor_of
    return jnp.minimum(jnp.maximum(drawn, -most), most).astype(held_as)


def setup_inputs(seed: int = 0) -> dict:
    splits = jax.random.split(jax.random.key(seed), 15)
    hidden_in = draw_hidden_in(jax.random.fold_in(splits[14], 71), 0)
    gain_attn = jnp.clip(1.0 + 0.1 * jax.random.normal(splits[1], (D,), jnp.float32), 0.5, 1.5)
    gain_ffn = jnp.clip(1.0 + 0.1 * jax.random.normal(splits[2], (D,), jnp.float32), 0.5, 1.5)
    w_query = scatter_about(splits[3], (D, HD), D ** -0.5, 0.125, ((1, 16),))
    w_key = scatter_about(splits[4], (D, HD), (28 * D) ** -0.5, 0.0234375, ((1, 16),))
    w_value = scatter_about(splits[5], (D, HD), D ** -0.5, 0.125, ((1, 16),))
    w_out = scatter_about(splits[6], (HD, D), (HD // 16) ** -0.5, 0.5, ((0, 16),))
    w_in = scatter_about(splits[7], (D, 2 * FF), D ** -0.5, 0.125, ((1, 16),))
    w_down = scatter_about(splits[8], (FF, D), FF ** -0.5, 0.078125, ((0, 16),))
    rel_bias = scatter_about(splits[9], (BUCKETS, HEADS), 1.0, 4.0, (), jnp.float32)
    kv_cache = draw_kv_cache(jax.random.fold_in(splits[14], 71), 0)
    segment_ids = draw_segment_ids(jax.random.fold_in(splits[14], 71), 0)
    kv_owner = draw_kv_owner(jax.random.fold_in(splits[14], 71), 0)
    kv_slot = draw_kv_slot(jax.random.fold_in(splits[14], 71), 0)
    return dict(hidden_in=hidden_in, gain_attn=gain_attn, gain_ffn=gain_ffn, w_query=w_query, w_key=w_key, w_value=w_value, w_out=w_out, w_in=w_in, w_down=w_down, rel_bias=rel_bias, kv_cache=kv_cache, segment_ids=segment_ids, kv_owner=kv_owner, kv_slot=kv_slot)


max_distance = 128
exact_range = 16
bucket_count = 32
glu_block = 64

def bucket_table():
    result = np.zeros(max_distance, np.int32)
    for distance in range(max_distance):
        if distance < exact_range:
            result[distance] = distance
        else:
            grown = math.log(distance / exact_range) / math.log(max_distance / exact_range) * (bucket_count - exact_range)
            result[distance] = min(bucket_count - 1, exact_range + int(grown))
    return result

def normalize(values_in, gain):
    widened = values_in.astype(jnp.float32)
    factor = lax.rsqrt(lax.optimization_barrier(jnp.mean(widened * widened, axis=1, keepdims=True)) + 1e-06)
    return (widened * factor * gain).astype(jnp.bfloat16)

def grouped_sum(left, right):
    row_count = left.shape[0]
    inner = left.shape[1] // N_GY
    parts = jnp.einsum('rgc,gcd->rgd', left.reshape(row_count, N_GY, inner).astype(jnp.float32), right.reshape(N_GY, inner, right.shape[1]).astype(jnp.float32))
    rounded = lax.optimization_barrier(parts.astype(jnp.bfloat16))
    return lax.optimization_barrier(jnp.sum(rounded.astype(jnp.float32), axis=1))

def attention(queries, keys_new, values_new, seg_ids, first_row, rel_bias, kv_cache, with_cache):
    row_count = queries.shape[0]
    buckets_of = jnp.asarray(bucket_table())
    row_ids = first_row + jnp.arange(row_count)
    positions = jnp.where(seg_ids >= 0, row_ids - seg_ids, 0) + jnp.where(seg_ids == 0, CACHE, 0)
    visible = (seg_ids[:, None] == seg_ids[None, :]) & (seg_ids[:, None] >= 0) & (positions[None, :] <= positions[:, None])
    visible = visible | jnp.eye(row_count, dtype=bool)
    buckets = buckets_of[jnp.clip(positions[:, None] - positions[None, :], 0, max_distance - 1)]
    key_heads = keys_new.reshape(row_count, HEADS, DK)
    value_heads = values_new.reshape(row_count, HEADS, DK)
    if with_cache:
        cache_pos = jnp.arange(CACHE)
        cache_visible = jnp.broadcast_to((seg_ids == 0)[:, None], (row_count, CACHE))
        cache_buckets = buckets_of[jnp.clip(positions[:, None] - cache_pos[None, :], 0, max_distance - 1)]
        visible = jnp.concatenate([cache_visible, visible], axis=1)
        buckets = jnp.concatenate([cache_buckets, buckets], axis=1)
        key_heads = jnp.concatenate([kv_cache[:, 0, :].reshape(CACHE, HEADS, DK), key_heads], axis=0)
        value_heads = jnp.concatenate([kv_cache[:, 1, :].reshape(CACHE, HEADS, DK), value_heads], axis=0)

    def one_head(head_item):
        head_query, head_key, head_value, head_bias = head_item
        scores = jnp.dot(head_query, head_key.T, preferred_element_type=jnp.float32) + head_bias[buckets]
        row_top = lax.optimization_barrier(jnp.max(jnp.where(visible, scores, -jnp.inf), axis=1, keepdims=True))
        weights = jnp.where(visible, jnp.exp(scores - row_top), 0.0)
        mixed_rows = jnp.dot(weights.astype(jnp.bfloat16), head_value, preferred_element_type=jnp.float32)
        return mixed_rows / lax.optimization_barrier(jnp.sum(weights, axis=1, keepdims=True))
    per_head = lax.map(one_head, (queries.reshape(row_count, HEADS, DK).transpose(1, 0, 2), key_heads.transpose(1, 0, 2), value_heads.transpose(1, 0, 2), rel_bias.T))
    return per_head.transpose(1, 0, 2).reshape(row_count, HEADS * DK).astype(jnp.bfloat16)

def reference(hidden_in, gain_attn, gain_ffn, w_query, w_key, w_value, w_out, w_in, w_down, rel_bias, kv_cache, segment_ids, kv_owner, kv_slot):
    outputs = []
    written = []
    for block_index in range(NEW // TOK_GX):
        row_start = block_index * TOK_GX
        x_block = hidden_in[row_start:row_start + TOK_GX]
        seg_ids = segment_ids[row_start:row_start + TOK_GX]
        x_norm = normalize(x_block, gain_attn)
        queries = jnp.dot(x_norm, w_query, preferred_element_type=jnp.float32).astype(jnp.bfloat16)
        keys_new = jnp.dot(x_norm, w_key, preferred_element_type=jnp.float32).astype(jnp.bfloat16)
        values_new = jnp.dot(x_norm, w_value, preferred_element_type=jnp.float32).astype(jnp.bfloat16)
        attended = attention(queries, keys_new, values_new, seg_ids, row_start, rel_bias, kv_cache, block_index == 0)
        residual = (x_block.astype(jnp.float32) + grouped_sum(attended, w_out)).astype(jnp.bfloat16)
        h_norm = normalize(residual, gain_ffn)
        gate_up = jnp.dot(h_norm, w_in, preferred_element_type=jnp.float32).reshape(TOK_GX, FF // glu_block, 2, glu_block)
        hidden = (jax.nn.gelu(gate_up[:, :, 0, :], approximate=True) * gate_up[:, :, 1, :]).reshape(TOK_GX, FF).astype(jnp.bfloat16)
        outputs.append(residual.astype(jnp.float32) + grouped_sum(hidden, w_down))
        written.append(jnp.stack([keys_new, values_new], axis=1))
    output = jnp.concatenate(outputs, axis=0)
    targets = kv_owner * TOK_GX + kv_slot
    kv_pool = jnp.zeros((NEW, 2, HD), jnp.bfloat16).at[targets].set(jnp.concatenate(written, axis=0))
    return (output, kv_pool)
```

```python
import math

import jax
import jax.numpy as jnp
import numpy as np
from jax import lax
from jax.experimental import pallas as pl
from jax.experimental.pallas import tpu as pltpu
from jax.sharding import PartitionSpec as P

DK = 64
CONT = 512
LANES = 128
TILE = 128
BLOCK = 256
PART_ROWS = CONT + 48

neg_big = -1e30
max_distance = 128
exact_range = 16
bucket_count = 32
VMEM_BYTES = 40 << 20


def bucket_table():
    result = np.zeros(max_distance, np.int32)
    for distance in range(max_distance):
        if distance < exact_range:
            result[distance] = distance
        else:
            grown = (
                math.log(distance / exact_range)
                / math.log(max_distance / exact_range)
                * (bucket_count - exact_range)
            )
            result[distance] = min(bucket_count - 1, exact_range + int(grown))
    return result


def bucket_starts():
    table = bucket_table()
    return [(int(b), int(np.argmax(table == b))) for b in range(1, bucket_count) if np.any(table == b)]


STARTS = bucket_starts()


def params(count=1):
    return pltpu.CompilerParams(
        dimension_semantics=("arbitrary",) * count, vmem_limit_bytes=VMEM_BYTES
    )


SMEM = pl.BlockSpec(memory_space=pltpu.SMEM)


def whole(shape):
    return pl.BlockSpec(shape, lambda *_: (0,) * len(shape))


def bias_tile(rel_bias, head, offset):
    lane = lax.broadcasted_iota(jnp.int32, (8, 2 * TILE), 1)
    distance = offset - jnp.where(lane < TILE, lane, lane - 2 * TILE)
    base = jnp.full((8, 2 * TILE), rel_bias[0, head], jnp.float32)
    for bucket, start in STARTS:
        base = jnp.where(distance >= start, rel_bias[bucket, head], base)
    rows = jnp.broadcast_to(base[:1], (TILE, 2 * TILE))
    return pltpu.roll(rows, 0, 1, stride=1, stride_axis=0)[:, :TILE]


def low_half(shape):
    return lax.broadcasted_iota(jnp.int32, shape, 1) < DK


def normed(chunk_refs, ids, gain, scratch):
    total = None
    for ref in chunk_refs:
        wide = ref[...].astype(jnp.float32)
        square = wide * wide
        total = square if total is None else total + square
    width = LANES * len(chunk_refs)
    factor = lax.rsqrt(jnp.sum(total, axis=1, keepdims=True) * (1.0 / width) + 1e-06)
    for position, ref in enumerate(chunk_refs):
        place = ids[position]
        at = pl.ds(pl.multiple_of(place * LANES, LANES), LANES)
        scratch[:, at] = (ref[...].astype(jnp.float32) * factor * gain[:, at]).astype(jnp.bfloat16)


def qkv_kernel(ids, *refs):
    chunks, (gain, w_q, w_k, w_v, q_out, k_out, v_out, scratch) = refs[:16], refs[16:]
    normed(chunks, ids, gain, scratch)
    x_norm = scratch[...]
    for weight, out in ((w_q, q_out), (w_k, k_out), (w_v, v_out)):
        out[...] = jnp.dot(x_norm, weight[...], preferred_element_type=jnp.float32).astype(
            jnp.bfloat16
        )


def project(ids, chunks, gain, w_query, w_key, w_value):
    rows = chunks[0].shape[0]
    width = gain.shape[1]
    row_block = pl.BlockSpec((BLOCK, LANES), lambda i: (i, 0))
    return pl.pallas_call(
        qkv_kernel,
        grid=(rows // BLOCK,),
        in_specs=[SMEM] + [row_block] * 16 + [whole((1, width))] + [whole((width, LANES))] * 3,
        out_specs=[row_block] * 3,
        out_shape=[jax.ShapeDtypeStruct((rows, LANES), jnp.bfloat16)] * 3,
        scratch_shapes=[pltpu.VMEM((BLOCK, width), jnp.bfloat16)],
        compiler_params=params(),
        name="norm_qkv",
    )(ids, *chunks, gain, w_query, w_key, w_value)


def two_heads(query):
    low = low_half(query.shape)
    zero = jnp.zeros_like(query)
    return jnp.concatenate([jnp.where(low, query, zero), jnp.where(low, zero, query)], axis=0)


def scores_of(queries, keys):
    return lax.dot_general(
        queries, keys, (((1,), (1,)), ((), ())), preferred_element_type=jnp.float32
    )


def soft(scores, values):
    rows = scores.shape[0] // 2
    top = jnp.max(scores, axis=1, keepdims=True)
    weights = jnp.exp(scores - top)
    total = jnp.sum(weights, axis=1, keepdims=True)
    mixed = jnp.dot(weights.astype(jnp.bfloat16), values, preferred_element_type=jnp.float32)
    mixed = mixed / total
    level = top + jnp.log(total)
    low = low_half((rows, LANES))
    return (
        jnp.where(low, mixed[:rows], mixed[rows:]),
        jnp.where(low, level[:rows], level[rows:]),
    )


def packed_kernel(place, rel_bias, query, keys, values, seg_col, seg_row, out, level_out, tiles):
    head_first = place[0]
    block = pl.program_id(0)
    rows, key_count = keys.shape[0] // 4, keys.shape[0]

    @pl.when(block == 0)
    def _():
        for head in range(2):
            for step in range(2):
                tiles[2 * head + step] = bias_tile(rel_bias, head_first + head, step * TILE)

    scores = scores_of(two_heads(query[...]), keys[...])
    far = [jnp.full((TILE, TILE), rel_bias[bucket_count - 1, head_first + h], jnp.float32) for h in range(2)]
    bias_rows = []
    for head in range(2):
        for part in range(BLOCK // TILE):
            row_tile = block * (BLOCK // TILE) + part
            pieces = []
            for column in range(key_count // TILE):
                near = jnp.where(row_tile == column, tiles[2 * head], tiles[2 * head + 1])
                close = (row_tile == column) | (row_tile == column + 1)
                pieces.append(jnp.where(close, near, far[head]))
            bias_rows.append(jnp.concatenate(pieces, axis=1))
    bias = jnp.concatenate(bias_rows, axis=0)
    row_ids = block * BLOCK + lax.broadcasted_iota(jnp.int32, (BLOCK, key_count), 0)
    col_ids = lax.broadcasted_iota(jnp.int32, (BLOCK, key_count), 1)
    own = seg_col[...]
    visible = ((own == seg_row[...]) & (own >= 0) & (col_ids <= row_ids)) | (col_ids == row_ids)
    hide = jnp.where(visible, 0.0, neg_big)
    hide = jnp.concatenate([hide, hide], axis=0)
    scores = jnp.where(hide == 0.0, scores + bias, neg_big)
    mixed, level = soft(scores, values[...])
    out[...] = mixed
    level_out[...] = level


def packed_attention(place, rel_bias, query, keys, values, seg_ids):
    rows = query.shape[0]
    row_block = pl.BlockSpec((BLOCK, LANES), lambda i: (i, 0))
    return pl.pallas_call(
        packed_kernel,
        grid=(rows // BLOCK,),
        in_specs=[
            SMEM,
            SMEM,
            row_block,
            whole((rows, LANES)),
            whole((rows, LANES)),
            pl.BlockSpec((BLOCK, 1), lambda i: (i, 0)),
            whole((1, rows)),
        ],
        out_specs=[row_block] * 2,
        out_shape=[jax.ShapeDtypeStruct((rows, LANES), jnp.float32)] * 2,
        scratch_shapes=[pltpu.VMEM((4, TILE, TILE), jnp.float32)],
        compiler_params=params(),
        name="packed_attention",
    )(place, rel_bias, query, keys, values, seg_ids.reshape(rows, 1), seg_ids.reshape(1, rows))


def cache_kernel(place, rel_bias, *refs):
    queries, (keys, values, out) = refs[:8], refs[8:]
    head_first, is_last = place[0], place[2]
    key_count = keys.shape[0]
    near = []
    for head in range(2):
        far = rel_bias[bucket_count - 1, head_first + head]
        tile = bias_tile(rel_bias, head_first + head, TILE)
        near.append(jnp.where(is_last == 1, tile, far))
    pieces = [[], [], []]
    for block in range(CONT // BLOCK):
        at = slice(block * BLOCK, (block + 1) * BLOCK)
        query = queries[0][at]
        for ref in queries[1:]:
            query = query + ref[at]
        scores = scores_of(two_heads(query), keys[...])
        bias_rows = []
        for head in range(2):
            far = rel_bias[bucket_count - 1, head_first + head]
            for part in range(BLOCK // TILE):
                last = near[head] if block == 0 and part == 0 else jnp.full((TILE, TILE), far, jnp.float32)
                body = jnp.full((TILE, key_count - TILE), far, jnp.float32)
                bias_rows.append(jnp.concatenate([body, last], axis=1))
        mixed, level = soft(scores + jnp.concatenate(bias_rows, axis=0), values[...])
        out[at] = mixed.astype(jnp.bfloat16)
        for part in range(BLOCK // TILE):
            turned = level[part * TILE : (part + 1) * TILE].T
            for head in range(2):
                left = turned[head * DK : head * DK + 1]
                for piece in range(3):
                    rounded = left.astype(jnp.bfloat16)
                    pieces[piece].append(rounded.astype(jnp.float32))
                    left = left - rounded.astype(jnp.float32)
    for piece in range(3):
        stack = jnp.concatenate(pieces[piece] + [jnp.zeros((8, LANES), jnp.float32)], axis=0)
        out[CONT + 16 * piece : CONT + 16 * (piece + 1)] = stack.astype(jnp.bfloat16)


def cache_attention(place, rel_bias, queries, keys, values):
    return pl.pallas_call(
        cache_kernel,
        in_specs=[SMEM, SMEM] + [pl.BlockSpec(memory_space=pltpu.VMEM)] * 10,
        out_specs=pl.BlockSpec(memory_space=pltpu.VMEM),
        out_shape=jax.ShapeDtypeStruct((PART_ROWS, LANES), jnp.bfloat16),
        compiler_params=pltpu.CompilerParams(vmem_limit_bytes=VMEM_BYTES),
        name="cache_attention",
    )(place, rel_bias, *queries, keys, values)


def spread_out(result, ids, scratch, outs):
    scratch[...] = result.astype(jnp.bfloat16)
    for position, out in enumerate(outs):
        for half in range(2):
            place = ids[2 * position + half]
            at = pl.ds(pl.multiple_of(place * LANES, LANES), LANES)
            out[half] = scratch[:, at]


def merge_kernel(ids, place, mixed, level, *refs):
    parts, w_out, outs, scratch, attended = refs[:8], refs[8], refs[9:17], refs[17], refs[18]
    block = pl.program_id(0)
    attended[...] = mixed[...].astype(jnp.bfloat16)

    @pl.when((place[1] == 0) & (block < CONT // BLOCK))
    def _():
        for part in range(BLOCK // TILE):
            row_at = pl.ds(pl.multiple_of(block * BLOCK + part * TILE, TILE), TILE)
            at = slice(part * TILE, (part + 1) * TILE)
            levels = [level[at]]
            rows = [mixed[at]]
            for ref in parts:
                held = (
                    ref[CONT : CONT + 16].astype(jnp.float32)
                    + ref[CONT + 16 : CONT + 32].astype(jnp.float32)
                    + ref[CONT + 32 : CONT + 48].astype(jnp.float32)
                )
                per_tile = CONT // TILE
                first = held[2 * part : 2 * part + 2]
                later = held[4 + 2 * part : 4 + 2 * part + 2]
                pair = jnp.where(block == 0, first, later)
                flat = jnp.concatenate(
                    [
                        jnp.broadcast_to(pair[0:1], (DK, LANES)),
                        jnp.broadcast_to(pair[1:2], (DK, LANES)),
                    ],
                    axis=0,
                )
                levels.append(flat.T)
                rows.append(ref[row_at].astype(jnp.float32))
            top = levels[0]
            for item in levels[1:]:
                top = jnp.maximum(top, item)
            total = jnp.zeros_like(top)
            summed = jnp.zeros_like(top)
            for item, row in zip(levels, rows):
                weight = jnp.exp(item - top)
                total = total + weight
                summed = summed + weight * row
            attended[at] = (summed / total).astype(jnp.bfloat16)

    result = jnp.dot(attended[...], w_out[...], preferred_element_type=jnp.float32)
    spread_out(result, ids, scratch, outs)


def merge_and_out(ids, place, mixed, level, parts, w_out):
    rows = mixed.shape[0]
    width = w_out.shape[1]
    row_block = pl.BlockSpec((BLOCK, LANES), lambda i: (i, 0))
    return pl.pallas_call(
        merge_kernel,
        grid=(rows // BLOCK,),
        in_specs=[SMEM, SMEM, row_block, row_block]
        + [whole((PART_ROWS, LANES))] * 8
        + [whole((LANES, width))],
        out_specs=[pl.BlockSpec((2, BLOCK, LANES), lambda i: (0, i, 0))] * 8,
        out_shape=[jax.ShapeDtypeStruct((2, rows, LANES), jnp.bfloat16)] * 8,
        scratch_shapes=[
            pltpu.VMEM((BLOCK, width), jnp.bfloat16),
            pltpu.VMEM((BLOCK, LANES), jnp.bfloat16),
        ],
        compiler_params=params(),
        name="merge_w_out",
    )(ids, place, mixed, level, *parts, w_out)


def gelu(value):
    inner = math.sqrt(2.0 / math.pi) * (value + 0.044715 * (value * value * value))
    return 0.5 * value * (1.0 + jnp.tanh(inner))


def ffn_kernel(ids, out_ids, *refs):
    chunks, gain, w_in, w_down = refs[:16], refs[16], refs[17], refs[18]
    outs, normed_rows, scratch = refs[19:27], refs[27], refs[28]
    normed(chunks, ids, gain, normed_rows)
    gate_up = jnp.dot(normed_rows[...], w_in[...], preferred_element_type=jnp.float32)
    pairs = gate_up.shape[1] // LANES
    low = low_half((BLOCK, LANES))
    hidden = []
    for first in range(0, pairs, 2):
        left = gate_up[:, first * LANES : (first + 1) * LANES]
        left_turned = pltpu.roll(left, DK, 1)
        if first + 1 < pairs:
            right = gate_up[:, (first + 1) * LANES : (first + 2) * LANES]
            right_turned = pltpu.roll(right, DK, 1)
            gate = jnp.where(low, left, right_turned)
            up = jnp.where(low, left_turned, right)
            hidden.append(gelu(gate) * up)
        else:
            hidden.append((gelu(left) * left_turned)[:, :DK])
    result = None
    start = 0
    for item in hidden:
        term = jnp.dot(
            item.astype(jnp.bfloat16),
            w_down[start : start + item.shape[1], :],
            preferred_element_type=jnp.float32,
        )
        result = term if result is None else result + term
        start += item.shape[1]
    spread_out(result, out_ids, scratch, outs)


def feed_forward(ids, out_ids, chunks, gain, w_in, w_down):
    rows = chunks[0].shape[0]
    width = gain.shape[1]
    row_block = pl.BlockSpec((BLOCK, LANES), lambda i: (i, 0))
    return pl.pallas_call(
        ffn_kernel,
        grid=(rows // BLOCK,),
        in_specs=[SMEM, SMEM]
        + [row_block] * 16
        + [whole((1, width)), whole(w_in.shape), whole(w_down.shape)],
        out_specs=[pl.BlockSpec((2, BLOCK, LANES), lambda i: (0, i, 0))] * 8,
        out_shape=[jax.ShapeDtypeStruct((2, rows, LANES), jnp.bfloat16)] * 8,
        scratch_shapes=[
            pltpu.VMEM((BLOCK, width), jnp.bfloat16),
            pltpu.VMEM((BLOCK, width), jnp.bfloat16),
        ],
        compiler_params=params(),
        name="norm_geglu",
    )(ids, out_ids, *chunks, gain, w_in, w_down)


def ordered_places(owner, me, owners):
    rows = owner.shape[1]
    relative = lax.rem(owner - me + owners, owners)
    which = lax.broadcasted_iota(jnp.int32, (owners, rows), 0)
    marks = (which == relative).astype(jnp.float32)
    before = lax.broadcasted_iota(jnp.int32, (rows, rows), 0) < lax.broadcasted_iota(
        jnp.int32, (rows, rows), 1
    )
    counts = jnp.dot(
        marks.astype(jnp.bfloat16),
        before.astype(jnp.float32).astype(jnp.bfloat16),
        preferred_element_type=jnp.float32,
    )
    rank = jnp.sum(marks * counts, axis=0, keepdims=True).astype(jnp.int32)
    return relative * (rows // owners) + rank


def selection(places):
    rows = places.shape[1]
    index = lax.broadcasted_iota(jnp.int32, (rows, rows), 0)
    return (index == places).astype(jnp.float32).astype(jnp.bfloat16)


def slots_kernel(place, owner, slot, places_out, slots_out):
    owners = slots_out.shape[0]
    rows = owner.shape[1]
    places = ordered_places(owner[...], place[1], owners)
    places_out[...] = places
    slots = slot[...]
    high = (slots // 32).astype(jnp.float32)
    low = (slots % 32).astype(jnp.float32)
    row_id = lax.broadcasted_iota(jnp.int32, (16, rows), 0)
    halves = jnp.where(row_id == 0, high, jnp.where(row_id == 1, low, 0.0)).astype(jnp.bfloat16)
    picked = scores_of(halves, selection(places))
    flat = picked[0:1] * 32.0 + picked[1:2]
    each = rows // owners
    for owner_id in range(owners):
        slots_out[owner_id : owner_id + 1, :] = flat[:, owner_id * each : (owner_id + 1) * each].astype(
            jnp.int32
        )


def order_slots(place, owner, slot, owners):
    rows = owner.shape[0]
    vmem = pl.BlockSpec(memory_space=pltpu.VMEM)
    return pl.pallas_call(
        slots_kernel,
        in_specs=[SMEM, vmem, vmem],
        out_specs=[vmem, vmem],
        out_shape=[
            jax.ShapeDtypeStruct((1, rows), jnp.int32),
            jax.ShapeDtypeStruct((owners, rows // owners), jnp.int32),
        ],
        compiler_params=pltpu.CompilerParams(vmem_limit_bytes=VMEM_BYTES),
        name="order_slots",
    )(place, owner.reshape(1, rows), slot.reshape(1, rows))


def order_rows_kernel(places, keys, values, *outs):
    picks = selection(places[...])
    each = keys.shape[0] // len(outs)
    for position, ref in enumerate((keys, values)):
        ordered = jnp.dot(picks, ref[...], preferred_element_type=jnp.float32).astype(jnp.bfloat16)
        for owner, out in enumerate(outs):
            out[position] = ordered[owner * each : (owner + 1) * each]


def order_rows(places, keys, values, owners):
    rows = keys.shape[0]
    vmem = pl.BlockSpec(memory_space=pltpu.VMEM)
    return pl.pallas_call(
        order_rows_kernel,
        in_specs=[vmem] * 3,
        out_specs=[vmem] * owners,
        out_shape=[jax.ShapeDtypeStruct((2, rows // owners, LANES), jnp.bfloat16)] * owners,
        compiler_params=pltpu.CompilerParams(vmem_limit_bytes=VMEM_BYTES),
        name="order_rows",
    )(places, keys, values)


def place_kernel(slots, *refs):
    received, (keys_out, values_out) = refs[:-2], refs[-2:]
    flat = jnp.concatenate([slots[i : i + 1] for i in range(slots.shape[0])], axis=1)
    picks = selection(flat)
    for position, out in enumerate((keys_out, values_out)):
        rows = jnp.concatenate([ref[position] for ref in received], axis=0)
        out[...] = jnp.dot(picks, rows, preferred_element_type=jnp.float32).astype(jnp.bfloat16)


def place_rows(slots, received):
    rows = slots.shape[0] * slots.shape[1]
    vmem = pl.BlockSpec(memory_space=pltpu.VMEM)
    return pl.pallas_call(
        place_kernel,
        in_specs=[vmem] * (1 + len(received)),
        out_specs=[vmem] * 2,
        out_shape=[jax.ShapeDtypeStruct((rows, LANES), jnp.bfloat16)] * 2,
        compiler_params=pltpu.CompilerParams(vmem_limit_bytes=VMEM_BYTES),
        name="place_rows",
    )(slots, *received)


def z_up(index):
    return (index + 4) % 16


def z_down(index):
    return (index + 12) % 16


def x_pair(index):
    return index ^ 2


def core_pair(index):
    return index ^ 1


def move(array, to):
    return lax.ppermute(array, "gy", [(index, to(index)) for index in range(16)])


def gathered_ids(gy):
    z, x, core = gy // 4, (gy // 2) % 2, gy % 2
    ids = []
    for other in range(2):
        for step in (0, 3, 1, 2):
            for across in range(2):
                ids.append(((z + step) % 4) * 4 + (x ^ across) * 2 + (core ^ other))
    return jnp.stack(ids).astype(jnp.int32)


def gather_chunks(own):
    across = move(own, x_pair)
    below = [move(own, z_up), move(across, z_up)]
    above = [move(own, z_down), move(across, z_down)]
    opposite = [move(below[0], z_up), move(above[1], z_down)]
    mine = [own, across] + below + above + opposite
    return mine + [move(item, core_pair) for item in mine]


Z_ORDER = (2, 1, 3, 0)


def scattered_ids(gy):
    z, x, core = gy // 4, (gy // 2) % 2, gy % 2
    ids = []
    for other in (1, 0):
        for step in Z_ORDER:
            for across in range(2):
                ids.append(((z + step) % 4) * 4 + (x ^ across) * 2 + (core ^ other))
    return jnp.stack(ids).astype(jnp.int32)


def wide(array):
    return array.astype(jnp.float32)


def added(*terms):
    total = wide(terms[0])
    for term in terms[1:]:
        total = total + wide(term)
    return total.astype(jnp.bfloat16)


def scatter_sum(pieces):
    held = {}
    for position, step in enumerate(Z_ORDER):
        sent, kept = pieces[position], pieces[4 + position]
        got = move(sent, core_pair)
        held[step] = [added(kept[half], got[half]) for half in range(2)]
    far_up = move(held[2][0], z_up)
    far_down = move(held[2][1], z_down)
    up = [move(added(held[1][0], far_up), z_up), move(held[1][1], z_up)]
    down = [move(held[3][0], z_down), move(added(held[3][1], far_down), z_down)]
    other = move(added(held[0][1], up[1], down[1]), x_pair)
    return wide(held[0][0]) + wide(up[0]) + wide(down[0]) + wide(other)


def shards(
    hidden_in,
    gain_attn,
    gain_ffn,
    w_query,
    w_key,
    w_value,
    w_out,
    w_in,
    w_down,
    rel_bias,
    kv_cache,
    segment_ids,
    kv_owner,
    kv_slot,
):
    gx_count = lax.axis_size("gx")
    gx, gy = lax.axis_index("gx"), lax.axis_index("gy")
    heads_here = w_query.shape[1] // DK
    place = jnp.stack([gy * heads_here, gx, (gx == gx_count - 1).astype(jnp.int32)]).astype(jnp.int32)
    in_ids, out_ids = gathered_ids(gy), scattered_ids(gy)
    places, slots_sent = order_slots(place, kv_owner, kv_slot, gx_count)
    cache_keys, cache_values = kv_cache[:, 0, :], kv_cache[:, 1, :]

    query, keys, values = project(
        in_ids, gather_chunks(hidden_in), gain_attn[None], w_query, w_key, w_value
    )
    first = jnp.where(gx == 0, query[:CONT], jnp.zeros_like(query[:CONT]))
    asked = [first] + [
        lax.ppermute(query[:CONT], "gx", [(0, index)]) for index in range(1, gx_count)
    ]
    mixed, level = packed_attention(place, rel_bias, query, keys, values, segment_ids)
    part = cache_attention(place, rel_bias, asked, cache_keys, cache_values)
    parts = [part] + [lax.ppermute(part, "gx", [(index, 0)]) for index in range(1, gx_count)]
    attn_part = scatter_sum(merge_and_out(out_ids, place, mixed, level, parts, w_out))
    h_shard = (wide(hidden_in) + attn_part).astype(jnp.bfloat16)
    ffn_part = scatter_sum(
        feed_forward(in_ids, out_ids, gather_chunks(h_shard), gain_ffn[None], w_in, w_down)
    )
    output = wide(h_shard) + ffn_part

    ordered = order_rows(places, keys, values, gx_count)

    def shifted(array, step):
        return lax.ppermute(
            array, "gx", [(index, (index + step) % gx_count) for index in range(gx_count)]
        )

    received = [ordered[0]] + [shifted(ordered[step], step) for step in range(1, gx_count)]
    got_slots = [slots_sent[:1]] + [
        shifted(slots_sent[step : step + 1], step) for step in range(1, gx_count)
    ]
    new_keys, new_values = place_rows(jnp.concatenate(got_slots, axis=0), received)
    return (output, jnp.stack([new_keys, new_values], axis=1))


def solution(mesh):
    placed = (
        P("gx", "gy"),
        P(),
        P(),
        P(None, "gy"),
        P(None, "gy"),
        P(None, "gy"),
        P("gy", None),
        P(None, "gy"),
        P("gy", None),
        P(),
        P("gx", None, "gy"),
        P("gx"),
        P("gx"),
        P("gx"),
    )
    return jax.shard_map(
        shards,
        mesh=mesh,
        in_specs=placed,
        out_specs=(P("gx", "gy"), P("gx", None, "gy")),
        check_vma=False,
    )
```
